128 devices in a mesh: pool: 2 (over core), pb: 8 (over y_hi, z), ka: 8 (over x, y_lo).
Axes of the slice: x: 4, y: 4 (y_hi: 2, y_lo: 2; y = y_hi * 2 + y_lo), z: 4, core: 2. Of those that a mesh axis runs over, the one named last changes fastest.
Arguments:
- tokens: bfloat16 [8192, 5376], P(('pb', 'ka'), 'pool'), may hold values from -16 to 16
- modality: int32 [8192], P('pb'), may hold values from 0 to 1, as said below
- proj_weight: bfloat16 [2, 5376, 4096], P('pool', None, 'ka'), may hold values from -0.078125 to 0.078125
- out_grad: bfloat16 [2, 8192, 1024], P('pool', 'pb', 'ka'), may hold values from -24 to 24
Outputs:
- grad_tokens: bfloat16 [8192, 5376], P(('pb', 'ka'), 'pool')
- grad_weight: float32 [2, 5376, 4096], P('pool', 'pb', 'ka')
The draws below stay inside these ranges and needn't reach their ends.
Inputs may be any that keep to these rules, and one draw needn't show every extreme that they name: `modality`: 1 marks image tokens; they stand in runs whose lengths are multiples of 256 except at the sequence's start and end, and both kinds occur.
All inputs are finite; a program needn't handle non-finite values.
Results may differ from the reference program's by a relative error of at most 0.018.
Values may be sent and summed in bfloat16 or wider, within the bound.
No kernel may reach another device: no remote copies, remote signals or barrier semaphores. Data moves between devices by JAX's collectives and lax.ppermute only.
A program may use at most 192 MiB of HBM per device.

```python
import math
import jax
import jax.numpy as jnp
from jax import lax

D = 5376
HD = 128
QPK = 2
IMG = 256
KV = 8
S = 8192
PW = 4096
N_PB = 8


def draw_modality(key, part):
    first_key, second_key = jax.random.split(jax.random.fold_in(key, 7))
    offset = jax.random.randint(first_key, (), 0, IMG)
    span_total = S // IMG + 2
    span_kinds = jax.random.randint(second_key, (span_total,), 0, 2)
    span_kinds = span_kinds.at[0].set(1).at[1].set(0)
    span_index = (jnp.arange(S, dtype=jnp.int32) + offset) // IMG
    return span_kinds[span_index].astype(jnp.int32)


def spiked(result, key, source, target, parts, factor):
    def block_of(position):
        return (jnp.arange(result.shape[position]) // (result.shape[position] // parts)).reshape((-1,) + (1,) * (result.ndim - 1 - position))

    first = jax.random.permutation(key, parts)[block_of(target)]
    second = (block_of(target) + parts // 2) % parts
    return jnp.where((block_of(source) == first) | (block_of(source) == second), factor * result, result)


def block_levels(stream_key, extent, pieces, smallest, largest):
    level = 1.0
    for position, shards_of in pieces:
        heights = jax.random.uniform(jax.random.fold_in(jax.random.fold_in(stream_key, 6), position), (shards_of,), jnp.float32, smallest / len(pieces), largest / len(pieces))
        level = level * jnp.repeat(jnp.exp(heights), extent[position] // shards_of).reshape((-1,) + (1,) * (len(extent) - 1 - position))
    return level


def noise(key, shape, width, most, cuts=(), kind=jnp.bfloat16):
    factor_of = block_levels(key, shape, cuts, -0.22, 0.18) if cuts else 1.0
    result = jax.random.normal(key, shape, jnp.float32) * width * factor_of
    return jnp.minimum(jnp.maximum(result, -most), most).astype(kind)


def heavy_noise(rng, extent, spread, reach, cuts, heavy, kind=jnp.bfloat16):
    drawn = spread * jax.random.normal(rng, extent, jnp.float32)
    if cuts:
        drawn = drawn * block_levels(rng, extent, cuts, -0.22, 0.18)
    return jnp.clip(spiked(drawn, jax.random.fold_in(rng, 3), *heavy), -reach, reach).astype(kind)


def setup_inputs(seed: int = 0) -> dict:
    arg_keys = jax.random.split(jax.random.key(seed), 5)
    return {
        "tokens": heavy_noise(arg_keys[0], (S, D), 1.0, 16.0, ((0, 64), (1, 2)), (0, 1, 64, 4.0)),
        "modality": draw_modality(jax.random.fold_in(arg_keys[4], 71), 0),
        "proj_weight": noise(arg_keys[2], (2, D, PW), D ** -0.5, 0.078125, ((0, 2), (2, 8))),
        "out_grad": noise(arg_keys[3], (QPK, S, KV * HD), 4.0, 24.0, ((0, 2), (1, 8), (2, 8))),
    }


def make_advance(key_rows, value_rows, scaling):
    contract_one = (((1,), (1,)), ((), ()))
    contract_zero = (((0,), (0,)), ((), ()))

    def advance(running, block_in):
        q_block, o_block = block_in
        scores = lax.dot_general(q_block, key_rows, contract_one, preferred_element_type=jnp.float32) * scaling
        row_max = lax.optimization_barrier(jnp.max(scores, axis=1, keepdims=True))
        log_total = row_max + jnp.log(lax.optimization_barrier(jnp.sum(jnp.exp(scores - row_max), axis=1, keepdims=True)))
        softmax = jnp.exp(scores - log_total)
        grad_prob = lax.dot_general(o_block, value_rows, contract_one, preferred_element_type=jnp.float32)
        delta = lax.optimization_barrier(jnp.sum(softmax * grad_prob, axis=1, keepdims=True))
        grad_score = (softmax * (grad_prob - delta)).astype(jnp.bfloat16)
        grad_query = jnp.dot(grad_score, key_rows, preferred_element_type=jnp.float32) * scaling
        key_part = lax.dot_general(grad_score, q_block, contract_zero, preferred_element_type=jnp.float32) * scaling
        value_part = lax.dot_general(softmax.astype(jnp.bfloat16), o_block, contract_zero, preferred_element_type=jnp.float32)
        key_low = lax.optimization_barrier(key_part.astype(jnp.bfloat16)).astype(jnp.float32)
        value_low = lax.optimization_barrier(value_part.astype(jnp.bfloat16)).astype(jnp.float32)
        return ((running[0] + key_low, running[1] + value_low), grad_query)
    return advance

def reference(tokens, modality, proj_weight, out_grad):
    scaling = 1.0 / math.sqrt(HD)
    group_width = (QPK + 2) * HD
    contract_one = (((1,), (1,)), ((), ()))
    contract_zero = (((0,), (0,)), ((), ()))
    is_image = (modality == 1)[:, None]
    text_proj = jnp.dot(tokens, proj_weight[0], preferred_element_type=jnp.float32)
    image_proj = jnp.dot(tokens, proj_weight[1], preferred_element_type=jnp.float32)
    projected = jnp.where(is_image, image_proj, text_proj).astype(jnp.bfloat16)
    block_rows = S // N_PB
    group_parts = []
    for group in range(KV):
        base = group * group_width
        key_rows = projected[:, base + QPK * HD:base + (QPK + 1) * HD]
        value_rows = projected[:, base + (QPK + 1) * HD:base + group_width]
        advance = make_advance(key_rows, value_rows, scaling)
        grad_keys = jnp.zeros((S, HD), jnp.float32)
        grad_values = jnp.zeros((S, HD), jnp.float32)
        head_grads = []
        for within in range(QPK):
            queries = projected[:, base + within * HD:base + (within + 1) * HD].reshape(N_PB, block_rows, HD)
            cotangent = out_grad[within, :, group * HD:(group + 1) * HD].reshape(N_PB, block_rows, HD)
            (grad_keys, grad_values), grad_query = lax.scan(advance, (grad_keys, grad_values), (queries, cotangent))
            head_grads.append(grad_query.reshape(S, HD))
        group_parts.append(jnp.concatenate(head_grads + [grad_keys, grad_values], axis=1))
    grad_proj = jnp.concatenate(group_parts, axis=1).astype(jnp.bfloat16)
    back_sum = jnp.zeros((S, D), jnp.float32)
    for group in range(KV):
        base = group * group_width
        grad_cols = grad_proj[:, base:base + group_width]
        back_text = lax.dot_general(grad_cols, proj_weight[0][:, base:base + group_width], contract_one, preferred_element_type=jnp.float32)
        back_image = lax.dot_general(grad_cols, proj_weight[1][:, base:base + group_width], contract_one, preferred_element_type=jnp.float32)
        chosen = jnp.where(is_image, back_image, back_text)
        back_sum = back_sum + lax.optimization_barrier(chosen.astype(jnp.bfloat16)).astype(jnp.float32)
    grad_tokens = back_sum.astype(jnp.bfloat16)
    text_part = jnp.where(is_image, jnp.zeros_like(grad_proj), grad_proj)
    image_part = jnp.where(is_image, grad_proj, jnp.zeros_like(grad_proj))
    text_weight = lax.dot_general(tokens, text_part, contract_zero, preferred_element_type=jnp.float32)
    image_weight = lax.dot_general(tokens, image_part, contract_zero, preferred_element_type=jnp.float32)
    grad_weight = jnp.stack([text_weight, image_weight])
    return (grad_tokens, grad_weight)
```

```python
import math

import jax
import jax.numpy as jnp
from jax import lax
from jax.experimental import pallas as pl
from jax.experimental.pallas import tpu as pltpu
from jax.sharding import Mesh, PartitionSpec as P


F32 = jnp.float32
BF16 = jnp.bfloat16
NT = (((1,), (1,)), ((), ()))
TN = (((0,), (0,)), ((), ()))
NN = (((1,), (0,)), ((), ()))
KEY_TILE = 512
Q_TILE = 512
ORDER = ((0, 0), (1, 0), (3, 0), (0, 1), (1, 1), (3, 1), (2, 0), (2, 1))


def shift(value, axis, step):
    count = lax.axis_size(axis)
    return lax.ppermute(value, axis, [(i, (i + step) % count) for i in range(count)])


def gather_parts(own, ring, pair):
    rows = own.shape[0]
    half = rows // 2
    third = rows * 3 // 8
    left = shift(own, ring, 1)
    right = shift(own, ring, -1)
    twin = shift(own, pair, 1)
    far_top = shift(left[:half], ring, 1)
    far_low = shift(right[half:], ring, -1)
    twin_left_top = shift(twin[:half], ring, 1)
    twin_right_low = shift(twin[half:], ring, -1)
    twin_left_low = shift(left[half:], pair, 1)
    twin_right_top = shift(right[:half], pair, 1)
    far = jnp.concatenate([far_top, far_low])
    twin_far_top = shift(twin_left_top[:third], ring, 1)
    twin_far_low = shift(twin_right_low[half - third :], ring, -1)
    twin_far_mid = shift(far[third : rows - third], pair, 1)
    return {
        (0, 0): own,
        (1, 0): right,
        (3, 0): left,
        (0, 1): twin,
        (1, 1): jnp.concatenate([twin_right_top, twin_right_low]),
        (3, 1): jnp.concatenate([twin_left_top, twin_left_low]),
        (2, 0): far,
        (2, 1): jnp.concatenate([twin_far_top, twin_far_mid, twin_far_low]),
    }


def widen(value):
    return value.astype(F32)


def reduce_ring(parts, ring):
    half = parts[0].shape[0] // 2
    far_top = shift(parts[2][:half], ring, 1)
    far_low = shift(parts[2][half:], ring, -1)
    next_low = shift(parts[1][half:], ring, 1)
    prev_top = shift(parts[3][:half], ring, -1)
    next_top = shift((widen(parts[1][:half]) + widen(far_top)).astype(BF16), ring, 1)
    prev_low = shift((widen(parts[3][half:]) + widen(far_low)).astype(BF16), ring, -1)
    top = widen(parts[0][:half]) + widen(next_top) + widen(prev_top)
    low = widen(parts[0][half:]) + widen(next_low) + widen(prev_low)
    return jnp.concatenate([top, low])


def reduce_parts(parts, ring, pair):
    twin = reduce_ring([parts[(d, 1)] for d in range(4)], ring)
    crossed = shift(twin.astype(BF16), pair, 1)
    own = reduce_ring([parts[(d, 0)] for d in range(4)], ring)
    return own + widen(crossed)


def relative(value, ring, pair):
    i = lax.axis_index(ring)
    j = lax.axis_index(pair)
    return {
        (d, e): lax.dynamic_slice_in_dim(
            lax.dynamic_slice_in_dim(value, (i + d) % 4, 1, 0), (j + e) % 2, 1, 1
        )[0, 0]
        for d, e in ORDER
    }


def stats_body(scale2, q_ref, o_ref, kv_ref, out_ref):
    step = pl.program_id(0)

    @pl.when(step == 0)
    def _():
        out_ref[0:1, :] = jnp.full((1, out_ref.shape[1]), -jnp.inf, F32)
        out_ref[1:8, :] = jnp.zeros((7, out_ref.shape[1]), F32)

    keys = kv_ref[:, :128]
    values = kv_ref[:, 128:]
    rows = q_ref.shape[0]
    for h in range(2):
        for b in range(rows // Q_TILE):
            at = slice(b * Q_TILE, (b + 1) * Q_TILE)
            lanes = slice(h * rows + b * Q_TILE, h * rows + (b + 1) * Q_TILE)
            s = lax.dot_general(keys, q_ref[at, h * 128 : (h + 1) * 128], NT, preferred_element_type=F32)
            g = lax.dot_general(values, o_ref[h, at, :], NT, preferred_element_type=F32)
            old = out_ref[0:1, lanes]
            new = jnp.maximum(old, jnp.max(s, axis=0, keepdims=True))
            fade = jnp.exp2((old - new) * scale2)
            e = jnp.exp2(s * scale2 - new * scale2)
            out_ref[0:1, lanes] = new
            out_ref[1:2, lanes] = fade * out_ref[1:2, lanes] + jnp.sum(e, axis=0, keepdims=True)
            out_ref[2:3, lanes] = fade * out_ref[2:3, lanes] + jnp.sum(e * g, axis=0, keepdims=True)


def grads_body(scale2, scaling, q_ref, o_ref, kv_ref, mine_ref, other_ref, dkv_ref, dq_ref, row_ref, acc_ref):
    step = pl.program_id(0)

    @pl.when(step == 0)
    def _():
        top_a = mine_ref[0:1, :]
        top_b = other_ref[0:1, :]
        top = jnp.maximum(top_a, top_b)
        fade_a = jnp.exp2((top_a - top) * scale2)
        fade_b = jnp.exp2((top_b - top) * scale2)
        total = mine_ref[1:2, :] * fade_a + other_ref[1:2, :] * fade_b
        mixed = mine_ref[2:3, :] * fade_a + other_ref[2:3, :] * fade_b
        row_ref[0:1, :] = top * scale2 + jnp.log2(total)
        row_ref[1:2, :] = mixed / total
        acc_ref[...] = jnp.zeros_like(acc_ref)

    keys = kv_ref[:, :128]
    values = kv_ref[:, 128:]
    keys_t = keys.T
    rows = q_ref.shape[0]
    dk = jnp.zeros((keys.shape[0], 128), F32)
    dv = jnp.zeros((keys.shape[0], 128), F32)
    for h in range(2):
        for b in range(rows // Q_TILE):
            at = slice(b * Q_TILE, (b + 1) * Q_TILE)
            lanes = slice(h * rows + b * Q_TILE, h * rows + (b + 1) * Q_TILE)
            q = q_ref[at, h * 128 : (h + 1) * 128]
            o = o_ref[h, at, :]
            s = lax.dot_general(keys, q, NT, preferred_element_type=F32)
            g = lax.dot_general(values, o, NT, preferred_element_type=F32)
            p = jnp.exp2(s * scale2 - row_ref[0:1, lanes])
            ds = (p * (g - row_ref[1:2, lanes])).astype(BF16)
            dv = dv + lax.dot_general(p.astype(BF16), o, NN, preferred_element_type=F32)
            dk = dk + lax.dot_general(ds, q, NN, preferred_element_type=F32)
            acc_ref[:, lanes] += lax.dot_general(keys_t, ds, NN, preferred_element_type=F32)
    dkv_ref[:, :128] = (dk * scaling).astype(BF16)
    dkv_ref[:, 128:] = dv.astype(BF16)

    @pl.when(step == pl.num_programs(0) - 1)
    def _():
        dq_ref[...] = (acc_ref[...] * scaling).astype(BF16)


def attention_stats(q, o, kv, scale2):
    count = kv.shape[0]
    total = 2 * q.shape[0]
    return pl.pallas_call(
        lambda *refs: stats_body(scale2, *refs),
        grid=(count // KEY_TILE,),
        in_specs=[
            pl.BlockSpec(q.shape, lambda i: (0, 0)),
            pl.BlockSpec(o.shape, lambda i: (0, 0, 0)),
            pl.BlockSpec((KEY_TILE, 256), lambda i: (i, 0)),
        ],
        out_specs=pl.BlockSpec((8, total), lambda i: (0, 0)),
        out_shape=jax.ShapeDtypeStruct((8, total), F32),
        name="attention_stats",
    )(q, o, kv)


def attention_grads(q, o, kv, mine, other, scale2, scaling):
    count = kv.shape[0]
    total = 2 * q.shape[0]
    return pl.pallas_call(
        lambda *refs: grads_body(scale2, scaling, *refs),
        grid=(count // KEY_TILE,),
        in_specs=[
            pl.BlockSpec(q.shape, lambda i: (0, 0)),
            pl.BlockSpec(o.shape, lambda i: (0, 0, 0)),
            pl.BlockSpec((KEY_TILE, 256), lambda i: (i, 0)),
            pl.BlockSpec(mine.shape, lambda i: (0, 0)),
            pl.BlockSpec(other.shape, lambda i: (0, 0)),
        ],
        out_specs=[
            pl.BlockSpec((KEY_TILE, 256), lambda i: (i, 0)),
            pl.BlockSpec((128, total), lambda i: (0, 0)),
        ],
        out_shape=[
            jax.ShapeDtypeStruct((count, 256), BF16),
            jax.ShapeDtypeStruct((128, total), BF16),
        ],
        scratch_shapes=[pltpu.VMEM((8, total), F32), pltpu.VMEM((128, total), F32)],
        name="attention_grads",
    )(q, o, kv, mine, other)


def shards(tokens, modality, proj_weight, out_grad):
    core = lax.axis_index("pool")
    head = out_grad.shape[2]
    scaling = 1.0 / math.sqrt(head)
    scale2 = scaling * math.log2(math.e)
    chunk, half_width = tokens.shape
    rows = 8 * chunk
    half_rows = rows // 2

    weight = proj_weight[0]
    w_own = lax.dynamic_slice_in_dim(weight, core * half_width, half_width, 0)
    w_other = shift(lax.dynamic_slice_in_dim(weight, (1 - core) * half_width, half_width, 0), "pool", 1)
    partner_grad = shift(out_grad[0], "pool", 1)

    parts = gather_parts(tokens, "x", "yl")

    kinds = relative(modality.reshape(4, 2, chunk), "x", "yl")
    kind = jnp.concatenate([kinds[k] for k in ORDER])
    owned = (kind == core)[:, None]
    cots = relative(
        jnp.concatenate([out_grad[0], partner_grad], axis=1).reshape(4, 2, chunk, 2 * head), "x", "yl"
    )
    cot = jnp.concatenate([cots[k] for k in ORDER])
    first = core == 0
    cot = jnp.stack(
        [
            jnp.where(first, cot[:, :head], cot[:, head:]),
            jnp.where(first, cot[:, head:], cot[:, :head]),
        ]
    )

    pieces = []
    blocks = []
    start = 0
    for keys in (ORDER[:4], ORDER[4:7], ORDER[7:]):
        block = jnp.concatenate([parts[k] for k in keys]) if len(keys) > 1 else parts[keys[0]]
        mask = owned[start : start + block.shape[0]]
        start += block.shape[0]
        pieces.append(
            jnp.where(
                mask,
                jnp.dot(block, w_own, preferred_element_type=F32),
                jnp.dot(block, w_other, preferred_element_type=F32),
            ).astype(BF16)
        )
        blocks.append(block)
    partial = jnp.concatenate(pieces)
    kv_part = partial[:, 2 * head :]
    kv_sent = shift(lax.dynamic_slice_in_dim(kv_part, (1 - core) * half_rows, half_rows, 0), "pool", 1)
    kv_mine = lax.dynamic_slice_in_dim(kv_part, core * half_rows, half_rows, 0)
    kv = (widen(kv_mine) + widen(kv_sent)).astype(BF16)
    q_part = partial[:, : 2 * head]
    q = (widen(q_part) + widen(shift(q_part, "pool", 1))).astype(BF16)

    kvs = gather_parts(kv, "z", "yh")
    kv_all = jnp.concatenate([kvs[k] for k in ORDER])
    mine = attention_stats(q, cot, kv_all, scale2)
    other = shift(mine, "pool", 1)
    dkv_all, dq_t = attention_grads(q, cot, kv_all, mine, other, scale2, scaling)

    half_tokens = jnp.concatenate(blocks)
    other_tokens = shift(half_tokens, "pool", 1)

    dq_t = widen(dq_t) + widen(shift(dq_t, "pool", 1))
    dq = dq_t.reshape(head, 2, rows).transpose(2, 1, 0).reshape(rows, 2 * head).astype(BF16)

    dkv_parts = {k: dkv_all[n * half_rows : (n + 1) * half_rows] for n, k in enumerate(ORDER)}
    dkv = reduce_parts(dkv_parts, "z", "yh").astype(BF16)
    dkv_other = shift(dkv, "pool", 1)
    dkv_rows = jnp.concatenate([jnp.where(first, dkv, dkv_other), jnp.where(first, dkv_other, dkv)])
    grad_proj = jnp.concatenate([dq, dkv_rows], axis=1)
    zero = jnp.zeros_like(grad_proj)
    grad_own = jnp.where(owned, grad_proj, zero)
    grad_other = jnp.where(owned, zero, grad_proj)

    back = (
        lax.dot_general(grad_own, w_own, NT, preferred_element_type=F32)
        + lax.dot_general(grad_other, w_other, NT, preferred_element_type=F32)
    ).astype(BF16)
    back_parts = {k: back[n * chunk : (n + 1) * chunk] for n, k in enumerate(ORDER)}
    grad_tokens = reduce_parts(back_parts, "x", "yl").astype(BF16)

    low = jnp.where(first, half_tokens, other_tokens)
    high = jnp.where(first, other_tokens, half_tokens)
    term = jnp.stack(
        [
            lax.dot_general(low, grad_own, TN, preferred_element_type=F32).astype(BF16),
            lax.dot_general(high, grad_own, TN, preferred_element_type=F32).astype(BF16),
        ]
    )
    term = term.reshape(2, 4, half_width // 4, 4 * head).transpose(1, 0, 2, 3)
    grad_weight = reduce_parts(relative(term, "z", "yh"), "z", "yh")
    return (grad_tokens, grad_weight[None])


def solution(mesh):
    fine = Mesh(mesh.devices.reshape(2, 2, 4, 4, 2), ("pool", "yh", "z", "x", "yl"))
    pb = ("yh", "z")
    ka = ("x", "yl")
    return jax.shard_map(
        shards,
        mesh=fine,
        in_specs=(P(pb + ka, "pool"), P(pb), P("pool", None, ka), P("pool", pb, ka)),
        out_specs=(P(pb + ka, "pool"), P("pool", pb, ka)),
        check_vma=False,
    )
```

```python
import math

import jax
import jax.numpy as jnp
from jax import lax
from jax.experimental import pallas as pl
from jax.experimental.pallas import tpu as pltpu
from jax.sharding import Mesh, PartitionSpec as P


F32 = jnp.float32
BF16 = jnp.bfloat16
NT = (((1,), (1,)), ((), ()))
TN = (((0,), (0,)), ((), ()))
NN = (((1,), (0,)), ((), ()))
KEY_TILE = 512
Q_TILE = 512
ORDER = ((0, 0), (1, 0), (3, 0), (0, 1), (1, 1), (3, 1), (2, 0), (2, 1))
tie = lax.optimization_barrier


def shift(value, axis, step):
    count = lax.axis_size(axis)
    return lax.ppermute(value, axis, [(i, (i + step) % count) for i in range(count)])


def widen(value):
    return value.astype(F32)


def join(*values):
    return jnp.concatenate(values)


def gather_rounds(own, ring, pair, work):
    rows = own.shape[0]
    h = rows // 2
    t = rows * 3 // 8
    parts = {(0, 0): own}
    left, right, twin = shift(own, ring, 1), shift(own, ring, -1), shift(own, pair, 1)
    carry = work(0, parts, None)
    left, right, twin, carry = tie((left, right, twin, carry))
    parts.update({(1, 0): right, (3, 0): left, (0, 1): twin})
    a = shift(join(left[:h], twin[:h]), ring, 1)
    b = shift(join(right[h:], twin[h:]), ring, -1)
    c = shift(join(left[h:], right[:h]), pair, 1)
    carry = work(1, parts, carry)
    a, b, c, carry = tie((a, b, c, carry))
    parts.update({(2, 0): join(a[:h], b[:h]), (1, 1): join(c[h:], b[h:]), (3, 1): join(a[h:], c[:h])})
    d = shift(a[h : h + t], ring, 1)
    e = shift(b[rows - t :], ring, -1)
    f = shift(join(a[t:h], b[: h - t]), pair, 1)
    carry = work(2, parts, carry)
    d, e, f, carry = tie((d, e, f, carry))
    parts[(2, 1)] = join(d, f, e)
    return parts, work(3, parts, carry)


def add(x, y):
    return (widen(x) + widen(y)).astype(BF16)


def scatter_one(p, ring):
    h = p[(2, 1)].shape[0] // 2
    ahead = shift(join(p[(2, 1)][:h], p[(1, 1)][h:]), ring, 1)
    back = shift(join(p[(2, 1)][h:], p[(3, 1)][:h]), ring, -1)
    return ahead, back


def scatter_two(p, got, ring):
    h = p[(2, 1)].shape[0] // 2
    ahead = shift(join(add(p[(1, 1)][:h], got[0][:h]), p[(2, 0)][:h]), ring, 1)
    back = shift(join(add(p[(3, 1)][h:], got[1][:h]), p[(2, 0)][h:]), ring, -1)
    return ahead, back


def scatter_three(p, first, got, ring, pair):
    h = p[(2, 1)].shape[0] // 2
    top = widen(p[(0, 1)][:h]) + widen(got[0][:h]) + widen(first[1][h:])
    low = widen(p[(0, 1)][h:]) + widen(got[1][:h]) + widen(first[0][h:])
    cross = shift(join(top, low).astype(BF16), pair, 1)
    ahead = shift(join(add(p[(1, 0)][:h], got[0][h:]), p[(1, 0)][h:]), ring, 1)
    back = shift(join(p[(3, 0)][:h], add(p[(3, 0)][h:], got[1][h:])), ring, -1)
    return cross, ahead, back


def scatter_sum(p, got):
    return widen(p[(0, 0)]) + widen(got[0]) + widen(got[1]) + widen(got[2])


def relative(value, ring, pair):
    i = lax.axis_index(ring)
    j = lax.axis_index(pair)
    return {
        (d, e): lax.dynamic_slice(
            value,
            ((i + d) % 4, (j + e) % 2) + (0,) * (value.ndim - 2),
            (1, 1) + value.shape[2:],
        )[0, 0]
        for d, e in ORDER
    }


def stats_body(scale2, fresh, q_ref, o_ref, kv_ref, *refs):
    out_ref = refs[-1]

    @pl.when(pl.program_id(0) == 0)
    def _():
        if fresh:
            out_ref[:, 0:1, :] = jnp.full((out_ref.shape[0], 1, Q_TILE), -jnp.inf, F32)
            out_ref[:, 1:8, :] = jnp.zeros((out_ref.shape[0], 7, Q_TILE), F32)
        else:
            out_ref[...] = refs[0][...]

    keys = kv_ref[:, :128]
    values = kv_ref[:, 128:]
    for b in range(out_ref.shape[0]):
        at = slice(b * Q_TILE, (b + 1) * Q_TILE)
        s = lax.dot_general(keys, q_ref[at, :], NT, preferred_element_type=F32)
        g = lax.dot_general(values, o_ref[at, :], NT, preferred_element_type=F32)
        old = out_ref[b, 0:1, :]
        new = jnp.maximum(old, jnp.max(s, axis=0, keepdims=True))
        fade = jnp.exp2((old - new) * scale2)
        e = jnp.exp2(s * scale2 - new * scale2)
        out_ref[b, 0:1, :] = new
        out_ref[b, 1:2, :] = fade * out_ref[b, 1:2, :] + jnp.sum(e, axis=0, keepdims=True)
        out_ref[b, 2:3, :] = fade * out_ref[b, 2:3, :] + jnp.sum(e * g, axis=0, keepdims=True)


def attention_stats(q, o, kv, scale2, running):
    count = kv.shape[0]
    blocks = q.shape[0] // Q_TILE
    shape = (blocks, 8, Q_TILE)
    whole = pl.BlockSpec(shape, lambda i: (0, 0, 0))
    fresh = running is None
    args = (q, o, kv) if fresh else (q, o, kv, running)
    return pl.pallas_call(
        lambda *refs: stats_body(scale2, fresh, *refs),
        grid=(count // KEY_TILE,),
        in_specs=[
            pl.BlockSpec(q.shape, lambda i: (0, 0)),
            pl.BlockSpec(o.shape, lambda i: (0, 0)),
            pl.BlockSpec((KEY_TILE, 256), lambda i: (i, 0)),
        ]
        + ([] if fresh else [whole]),
        out_specs=whole,
        out_shape=jax.ShapeDtypeStruct(shape, F32),
        name="attention_stats",
    )(*args)


def grads_body(scale2, scaling, fresh, q_ref, o_ref, kv_ref, mine_ref, other_ref, *refs):
    dkv_ref, dq_ref, row_ref = refs[-3:]

    @pl.when(pl.program_id(0) == 0)
    def _():
        for b in range(dq_ref.shape[0]):
            top_a = mine_ref[b, 0:1, :]
            top_b = other_ref[b, 0:1, :]
            top = jnp.maximum(top_a, top_b)
            fade_a = jnp.exp2((top_a - top) * scale2)
            fade_b = jnp.exp2((top_b - top) * scale2)
            total = mine_ref[b, 1:2, :] * fade_a + other_ref[b, 1:2, :] * fade_b
            mixed = mine_ref[b, 2:3, :] * fade_a + other_ref[b, 2:3, :] * fade_b
            row_ref[b, 0:1, :] = top * scale2 + jnp.log2(total)
            row_ref[b, 1:2, :] = mixed / total
        if fresh:
            dq_ref[...] = jnp.zeros_like(dq_ref)
        else:
            dq_ref[...] = refs[0][...]

    keys = kv_ref[:, :128]
    values = kv_ref[:, 128:]
    keys_t = keys.T
    dk = jnp.zeros((keys.shape[0], 128), F32)
    dv = jnp.zeros((keys.shape[0], 128), F32)
    for b in range(dq_ref.shape[0]):
        at = slice(b * Q_TILE, (b + 1) * Q_TILE)
        q = q_ref[at, :]
        o = o_ref[at, :]
        s = lax.dot_general(keys, q, NT, preferred_element_type=F32)
        g = lax.dot_general(values, o, NT, preferred_element_type=F32)
        p = jnp.exp2(s * scale2 - row_ref[b, 0:1, :])
        ds = (p * (g - row_ref[b, 1:2, :])).astype(BF16)
        dv = dv + lax.dot_general(p.astype(BF16), o, NN, preferred_element_type=F32)
        dk = dk + lax.dot_general(ds, q, NN, preferred_element_type=F32)
        dq_ref[b] += lax.dot_general(keys_t, ds, NN, preferred_element_type=F32)
    dkv_ref[:, :128] = (dk * scaling).astype(BF16)
    dkv_ref[:, 128:] = dv.astype(BF16)


def attention_grads(q, o, kv, mine, other, scale2, scaling, running):
    count = kv.shape[0]
    blocks = q.shape[0] // Q_TILE
    shape = (blocks, 128, Q_TILE)
    fresh = running is None
    stats = pl.BlockSpec(mine.shape, lambda i: (0, 0, 0))
    whole = pl.BlockSpec(shape, lambda i: (0, 0, 0))
    args = (q, o, kv, mine, other) + (() if fresh else (running,))
    return pl.pallas_call(
        lambda *refs: grads_body(scale2, scaling, fresh, *refs),
        grid=(count // KEY_TILE,),
        in_specs=[
            pl.BlockSpec(q.shape, lambda i: (0, 0)),
            pl.BlockSpec(o.shape, lambda i: (0, 0)),
            pl.BlockSpec((KEY_TILE, 256), lambda i: (i, 0)),
            stats,
            stats,
        ]
        + ([] if fresh else [whole]),
        out_specs=[pl.BlockSpec((KEY_TILE, 256), lambda i: (i, 0)), whole],
        out_shape=[
            jax.ShapeDtypeStruct((count, 256), BF16),
            jax.ShapeDtypeStruct(shape, F32),
        ],
        scratch_shapes=[pltpu.VMEM((blocks, 8, Q_TILE), F32)],
        name="attention_grads",
    )(*args)


def chosen_body(dims, flags, x_ref, mask_ref, own_ref, other_ref, out_ref):
    i = pl.program_id(0)

    @pl.when(flags[i, 0] > 0)
    def _():
        out_ref[...] = lax.dot_general(
            x_ref[...], own_ref[...], dims, preferred_element_type=F32
        ).astype(BF16)

    @pl.when(flags[i, 1] > 0)
    def _():
        result = lax.dot_general(
            x_ref[...], other_ref[...], dims, preferred_element_type=F32
        ).astype(BF16)
        out_ref[...] = jnp.where(mask_ref[...] > 0, out_ref[...], result)


def chosen_dot(x, mask, flags, own, other, dims, chunk):
    rows, width = x.shape
    out_width = own.shape[1] if dims is NN else own.shape[0]
    return pl.pallas_call(
        lambda *refs: chosen_body(dims, *refs),
        grid_spec=pltpu.PrefetchScalarGridSpec(
            num_scalar_prefetch=1,
            grid=(rows // chunk,),
            in_specs=[
                pl.BlockSpec((chunk, width), lambda i, f: (i, 0)),
                pl.BlockSpec((chunk, 1), lambda i, f: (i, 0)),
                pl.BlockSpec(own.shape, lambda i, f: (0, 0)),
                pl.BlockSpec(other.shape, lambda i, f: (0, 0)),
            ],
            out_specs=pl.BlockSpec((chunk, out_width), lambda i, f: (i, 0)),
        ),
        out_shape=jax.ShapeDtypeStruct((rows, out_width), BF16),
        name="chosen_dot",
    )(flags, x, mask, own, other)


def shards(tokens, modality, proj_weight, out_grad):
    core = lax.axis_index("pool")
    first = core == 0
    head = out_grad.shape[2]
    scaling = 1.0 / math.sqrt(head)
    scale2 = scaling * math.log2(math.e)
    chunk, half_width = tokens.shape
    rows = 8 * chunk
    half_rows = rows // 2

    weight = proj_weight[0]
    w_own = lax.dynamic_slice_in_dim(weight, core * half_width, half_width, 0)
    w_other = shift(lax.dynamic_slice_in_dim(weight, (1 - core) * half_width, half_width, 0), "pool", 1)
    partner_grad = shift(out_grad[0], "pool", 1)

    kinds = relative(modality.reshape(4, 2, chunk), "x", "yl")
    owned = {k: (kinds[k] == core).astype(jnp.int32) for k in ORDER}

    def flags_of(keys):
        some = jnp.stack([jnp.max(owned[k]) for k in keys])
        none = jnp.stack([jnp.max(1 - owned[k]) for k in keys])
        return jnp.stack([some, none], axis=1)

    def mask_of(keys):
        return jnp.concatenate([owned[k] for k in keys])[:, None]

    def project(keys, parts):
        x = jnp.concatenate([parts[k] for k in keys]) if len(keys) > 1 else parts[keys[0]]
        return x, chosen_dot(x, mask_of(keys), flags_of(keys), w_own, w_other, NN, chunk)

    groups = (ORDER[:4], ORDER[4:7], ORDER[7:])

    def token_work(n, parts, carry):
        if n == 0:
            return ()
        return carry + (project(groups[n - 1], parts),)

    parts, done = gather_rounds(tokens, "x", "yl", token_work)
    half_tokens = jnp.concatenate([x for x, _ in done])
    partial = jnp.concatenate([y for _, y in done])
    cots = relative(
        jnp.concatenate([out_grad[0], partner_grad], axis=1).reshape(4, 2, chunk, 2 * head), "x", "yl"
    )
    cot = jnp.concatenate([cots[k] for k in ORDER])
    cot = jnp.concatenate(
        [
            jnp.where(first, cot[:, :head], cot[:, head:]),
            jnp.where(first, cot[:, head:], cot[:, :head]),
        ]
    )

    kv_part = partial[:, 2 * head :]
    kv_sent = shift(lax.dynamic_slice_in_dim(kv_part, (1 - core) * half_rows, half_rows, 0), "pool", 1)
    kv_mine = lax.dynamic_slice_in_dim(kv_part, core * half_rows, half_rows, 0)
    kv = add(kv_mine, kv_sent)
    q_part = jnp.concatenate([partial[:, :head], partial[:, head : 2 * head]])
    q = add(q_part, shift(q_part, "pool", 1))

    def key_work(n, kvs, carry):
        if n == 0:
            return attention_stats(q, cot, kvs[(0, 0)], scale2, None)
        keys = (ORDER[1:4], ORDER[4:7], ORDER[7:])[n - 1]
        block = jnp.concatenate([kvs[k] for k in keys]) if len(keys) > 1 else kvs[keys[0]]
        return attention_stats(q, cot, block, scale2, carry)

    kvs, mine = gather_rounds(kv, "z", "yh", key_work)
    other = shift(mine, "pool", 1)
    other_tokens = shift(half_tokens, "pool", 1)

    def key_grads(keys, running):
        block = jnp.concatenate([kvs[k] for k in keys])
        dkv, dq = attention_grads(q, cot, block, mine, other, scale2, scaling, running)
        return {k: dkv[n * half_rows : (n + 1) * half_rows] for n, k in enumerate(keys)}, dq

    pieces, dq_t = key_grads(((2, 1), (1, 1), (3, 1)), None)
    got_one = scatter_one(pieces, "z")
    more, dq_t = key_grads(((2, 0), (1, 0), (3, 0)), dq_t)
    pieces.update(more)
    got_one, dq_t = tie((got_one, dq_t))
    got_two = scatter_two(pieces, got_one, "z")
    more, dq_t = key_grads(((0, 1), (0, 0)), dq_t)
    pieces.update(more)
    got_two, dq_t = tie((got_two, dq_t))
    dq_t = (dq_t * scaling).astype(BF16)
    dq_sent = shift(dq_t, "pool", 1)
    got_three = scatter_three(pieces, got_one, got_two, "z", "yh")
    dq_t = (widen(dq_t) + widen(dq_sent)).reshape(2, rows // Q_TILE, head, Q_TILE)
    dq = dq_t.transpose(1, 3, 0, 2).reshape(rows, 2 * head).astype(BF16)
    got_three, dq = tie((got_three, dq))
    dkv = scatter_sum(pieces, got_three).astype(BF16)
    dkv_other = shift(dkv, "pool", 1)
    dkv_rows = jnp.concatenate([jnp.where(first, dkv, dkv_other), jnp.where(first, dkv_other, dkv)])
    grad_proj = jnp.concatenate([dq, dkv_rows], axis=1)
    grad_own = jnp.where(mask_of(ORDER) > 0, grad_proj, jnp.zeros_like(grad_proj))

    def back_of(keys):
        at = [ORDER.index(k) for k in keys]
        g = jnp.concatenate([grad_proj[n * chunk : (n + 1) * chunk] for n in at])
        out = chosen_dot(g, mask_of(keys), flags_of(keys), w_own, w_other, NT, chunk)
        return {k: out[n * chunk : (n + 1) * chunk] for n, k in enumerate(keys)}

    def term_of(twin):
        half = (lax.axis_index("yh") + twin) % 2
        x = jnp.where(half == core, half_tokens, other_tokens)
        term = lax.dot_general(x, grad_own, TN, preferred_element_type=F32).astype(BF16)
        term = term.reshape(4, half_width // 4, 4 * head)
        i = lax.axis_index("z")
        return {
            (d, twin): lax.dynamic_index_in_dim(term, (i + d) % 4, 0, keepdims=False) for d in range(4)
        }

    back = back_of(((2, 1), (1, 1), (3, 1)))
    term = term_of(1)
    back_one = scatter_one(back, "x")
    term_one = scatter_one(term, "z")
    more_back = back_of(((2, 0), (0, 1), (1, 0), (3, 0), (0, 0)))
    more_term = term_of(0)
    back_one, term_one, more_back, more_term = tie((back_one, term_one, more_back, more_term))
    back.update(more_back)
    term.update(more_term)
    back_two = scatter_two(back, back_one, "x")
    term_two = scatter_two(term, term_one, "z")
    back_two, term_two = tie((back_two, term_two))
    back_three = scatter_three(back, back_one, back_two, "x", "yl")
    term_three = scatter_three(term, term_one, term_two, "z", "yh")
    back_three, term_three = tie((back_three, term_three))
    grad_tokens = scatter_sum(back, back_three).astype(BF16)
    grad_weight = scatter_sum(term, term_three)
    return (grad_tokens, grad_weight[None])


def solution(mesh):
    fine = Mesh(mesh.devices.reshape(2, 2, 4, 4, 2), ("pool", "yh", "z", "x", "yl"))
    pb = ("yh", "z")
    ka = ("x", "yl")
    return jax.shard_map(
        shards,
        mesh=fine,
        in_specs=(P(pb + ka, "pool"), P(pb), P("pool", None, ka), P("pool", pb, ka)),
        out_specs=(P(pb + ka, "pool"), P("pool", pb, ka)),
        check_vma=False,
    )
```

```python
import math

import jax
import jax.numpy as jnp
from jax import lax
from jax.experimental import pallas as pl
from jax.experimental.pallas import tpu as pltpu
from jax.sharding import Mesh, PartitionSpec as P


F32 = jnp.float32
BF16 = jnp.bfloat16
NT = (((1,), (1,)), ((), ()))
TN = (((0,), (0,)), ((), ()))
NN = (((1,), (0,)), ((), ()))
KEY_TILE = 512
Q_TILE = 512
UNROLL = 1
ORDER = ((0, 0), (1, 0), (3, 0), (0, 1), (2, 0), (1, 1), (3, 1), (2, 1))
tie = lax.optimization_barrier


def shift(value, axis, step):
    count = lax.axis_size(axis)
    return lax.ppermute(value, axis, [(i, (i + step) % count) for i in range(count)])


def widen(value):
    return value.astype(F32)


def join(*values):
    return jnp.concatenate(values)


def gather_rounds(own, ring, pair, work):
    rows = own.shape[0]
    h = rows // 2
    t = rows * 3 // 8
    parts = {(0, 0): own}
    left, right, twin = shift(own, ring, 1), shift(own, ring, -1), shift(own, pair, 1)
    carry = work(0, parts, None)
    left, right, twin, carry = tie((left, right, twin, carry))
    parts.update({(1, 0): right, (3, 0): left, (0, 1): twin})
    a = shift(join(left[:h], twin[:h]), ring, 1)
    b = shift(join(right[h:], twin[h:]), ring, -1)
    c = shift(join(left[h:], right[:h]), pair, 1)
    carry = work(1, parts, carry)
    a, b, c, carry = tie((a, b, c, carry))
    parts.update({(2, 0): join(a[:h], b[:h]), (1, 1): join(c[h:], b[h:]), (3, 1): join(a[h:], c[:h])})
    d = shift(a[h : h + t], ring, 1)
    e = shift(b[rows - t :], ring, -1)
    f = shift(join(a[t:h], b[: h - t]), pair, 1)
    carry = work(2, parts, carry)
    d, e, f, carry = tie((d, e, f, carry))
    parts[(2, 1)] = join(d, f, e)
    return parts, work(3, parts, carry)


def add(x, y):
    return (widen(x) + widen(y)).astype(BF16)


def scatter_one(p, ring):
    h = p[(2, 1)].shape[0] // 2
    ahead = shift(join(p[(2, 1)][:h], p[(1, 1)][h:]), ring, 1)
    back = shift(join(p[(2, 1)][h:], p[(3, 1)][:h]), ring, -1)
    return ahead, back


def scatter_two(p, got, ring):
    h = p[(2, 1)].shape[0] // 2
    ahead = shift(join(add(p[(1, 1)][:h], got[0][:h]), p[(2, 0)][:h]), ring, 1)
    back = shift(join(add(p[(3, 1)][h:], got[1][:h]), p[(2, 0)][h:]), ring, -1)
    return ahead, back


def scatter_three(p, first, got, ring, pair):
    h = p[(2, 1)].shape[0] // 2
    top = widen(p[(0, 1)][:h]) + widen(got[0][:h]) + widen(first[1][h:])
    low = widen(p[(0, 1)][h:]) + widen(got[1][:h]) + widen(first[0][h:])
    cross = shift(join(top, low).astype(BF16), pair, 1)
    ahead = shift(join(add(p[(1, 0)][:h], got[0][h:]), p[(1, 0)][h:]), ring, 1)
    back = shift(join(p[(3, 0)][:h], add(p[(3, 0)][h:], got[1][h:])), ring, -1)
    return cross, ahead, back


def scatter_sum(p, got):
    return widen(p[(0, 0)]) + widen(got[0]) + widen(got[1]) + widen(got[2])


def stats_body(scale2, fresh, q_ref, o_ref, kv_ref, *refs):
    out_ref = refs[-1]

    @pl.when(pl.program_id(0) == 0)
    def _():
        if fresh:
            out_ref[:, 0:1, :] = jnp.full((out_ref.shape[0], 1, Q_TILE), -jnp.inf, F32)
            out_ref[:, 1:8, :] = jnp.zeros((out_ref.shape[0], 7, Q_TILE), F32)
        else:
            out_ref[...] = refs[0][...]

    keys = kv_ref[:, :128]
    values = kv_ref[:, 128:]

    def block(b, _):
        at = pl.ds(pl.multiple_of(b * Q_TILE, Q_TILE), Q_TILE)
        s = lax.dot_general(keys, q_ref[at, :], NT, preferred_element_type=F32)
        g = lax.dot_general(values, o_ref[at, :], NT, preferred_element_type=F32)
        old = out_ref[b, 0:1, :]
        new = jnp.maximum(old, jnp.max(s, axis=0, keepdims=True))
        fade = jnp.exp2((old - new) * scale2)
        e = jnp.exp2(s * scale2 - new * scale2)
        out_ref[b, 0:1, :] = new
        out_ref[b, 1:2, :] = fade * out_ref[b, 1:2, :] + jnp.sum(e, axis=0, keepdims=True)
        out_ref[b, 2:3, :] = fade * out_ref[b, 2:3, :] + jnp.sum(e * g, axis=0, keepdims=True)
        return _

    lax.fori_loop(0, out_ref.shape[0], block, 0, unroll=UNROLL)


def attention_stats(q, o, kv, scale2, running):
    count = kv.shape[0]
    blocks = q.shape[0] // Q_TILE
    shape = (blocks, 8, Q_TILE)
    whole = pl.BlockSpec(shape, lambda i: (0, 0, 0))
    fresh = running is None
    args = (q, o, kv) if fresh else (q, o, kv, running)
    return pl.pallas_call(
        lambda *refs: stats_body(scale2, fresh, *refs),
        grid=(count // KEY_TILE,),
        in_specs=[
            pl.BlockSpec(q.shape, lambda i: (0, 0)),
            pl.BlockSpec(o.shape, lambda i: (0, 0)),
            pl.BlockSpec((KEY_TILE, 256), lambda i: (i, 0)),
        ]
        + ([] if fresh else [whole]),
        out_specs=whole,
        out_shape=jax.ShapeDtypeStruct(shape, F32),
        name="attention_stats",
    )(*args)


def grads_body(scale2, scaling, fresh, q_ref, o_ref, kv_ref, mine_ref, other_ref, *refs):
    dkv_ref, dq_ref, row_ref, acc_ref = refs[-4:]

    @pl.when(pl.program_id(0) == 0)
    def _():
        for b in range(dq_ref.shape[0]):
            top_a = mine_ref[b, 0:1, :]
            top_b = other_ref[b, 0:1, :]
            top = jnp.maximum(top_a, top_b)
            fade_a = jnp.exp2((top_a - top) * scale2)
            fade_b = jnp.exp2((top_b - top) * scale2)
            total = mine_ref[b, 1:2, :] * fade_a + other_ref[b, 1:2, :] * fade_b
            mixed = mine_ref[b, 2:3, :] * fade_a + other_ref[b, 2:3, :] * fade_b
            row_ref[b, 0:1, :] = top * scale2 + jnp.log2(total)
            row_ref[b, 1:2, :] = mixed / total
        if fresh:
            dq_ref[...] = jnp.zeros_like(dq_ref)
        else:
            dq_ref[...] = refs[0][...]

    keys = kv_ref[:, :128]
    values = kv_ref[:, 128:]
    keys_t = keys.T
    acc_ref[...] = jnp.zeros_like(acc_ref)

    def block(b, _):
        at = pl.ds(pl.multiple_of(b * Q_TILE, Q_TILE), Q_TILE)
        q = q_ref[at, :]
        o = o_ref[at, :]
        s = lax.dot_general(keys, q, NT, preferred_element_type=F32)
        g = lax.dot_general(values, o, NT, preferred_element_type=F32)
        p = jnp.exp2(s * scale2 - row_ref[b, 0:1, :])
        ds = (p * (g - row_ref[b, 1:2, :])).astype(BF16)
        acc_ref[:, :128] += lax.dot_general(ds, q, NN, preferred_element_type=F32)
        acc_ref[:, 128:] += lax.dot_general(p.astype(BF16), o, NN, preferred_element_type=F32)
        dq_ref[b] += lax.dot_general(keys_t, ds, NN, preferred_element_type=F32)
        return _

    lax.fori_loop(0, dq_ref.shape[0], block, 0, unroll=UNROLL)
    dkv_ref[:, :128] = (acc_ref[:, :128] * scaling).astype(BF16)
    dkv_ref[:, 128:] = acc_ref[:, 128:].astype(BF16)


def attention_grads(q, o, kv, tiles, mine, other, scale2, scaling, running):
    start, count = tiles.start, len(tiles) * KEY_TILE
    blocks = q.shape[0] // Q_TILE
    shape = (blocks, 128, Q_TILE)
    fresh = running is None
    stats = pl.BlockSpec(mine.shape, lambda i: (0, 0, 0))
    whole = pl.BlockSpec(shape, lambda i: (0, 0, 0))
    args = (q, o, kv, mine, other) + (() if fresh else (running,))
    return pl.pallas_call(
        lambda *refs: grads_body(scale2, scaling, fresh, *refs),
        grid=(count // KEY_TILE,),
        in_specs=[
            pl.BlockSpec(q.shape, lambda i: (0, 0)),
            pl.BlockSpec(o.shape, lambda i: (0, 0)),
            pl.BlockSpec((KEY_TILE, 256), lambda i: (i + start, 0)),
            stats,
            stats,
        ]
        + ([] if fresh else [whole]),
        out_specs=[pl.BlockSpec((KEY_TILE, 256), lambda i: (i, 0)), whole],
        out_shape=[
            jax.ShapeDtypeStruct((count, 256), BF16),
            jax.ShapeDtypeStruct(shape, F32),
        ],
        scratch_shapes=[pltpu.VMEM((blocks, 8, Q_TILE), F32), pltpu.VMEM((KEY_TILE, 256), F32)],
        name="attention_grads",
    )(*args)


def rolled(value, ring, pair):
    i = lax.axis_index(ring)
    j = lax.axis_index(pair)
    value = lax.dynamic_slice_in_dim(jnp.concatenate([value, value]), i, 4, 0)
    value = lax.dynamic_slice_in_dim(jnp.concatenate([value, value], axis=1), j, 2, 1)
    return jnp.stack([value[k] for k in ORDER])


def shards(tokens, modality, proj_weight, out_grad):
    core = lax.axis_index("pool")
    first = core == 0
    head = out_grad.shape[2]
    scaling = 1.0 / math.sqrt(head)
    scale2 = scaling * math.log2(math.e)
    chunk, half_width = tokens.shape
    rows = 8 * chunk
    half_rows = rows // 2

    weight = proj_weight[0]
    w_own = lax.dynamic_slice_in_dim(weight, core * half_width, half_width, 0)
    w_other = shift(lax.dynamic_slice_in_dim(weight, (1 - core) * half_width, half_width, 0), "pool", 1)
    partner_grad = shift(out_grad[0], "pool", 1)

    owned = (rolled(modality.reshape(4, 2, chunk), "x", "yl").reshape(rows) == core)[:, None]

    def project(at, parts):
        x = join(*[parts[k] for k in ORDER[at]])
        return x, jnp.where(
            owned[at.start * chunk : at.stop * chunk],
            jnp.dot(x, w_own, preferred_element_type=F32),
            jnp.dot(x, w_other, preferred_element_type=F32),
        ).astype(BF16)

    groups = (slice(0, 4), slice(4, 7), slice(7, 8))

    def token_work(n, parts, carry):
        if n == 0:
            cots = rolled(
                jnp.concatenate([out_grad[0], partner_grad], axis=1).reshape(4, 2, chunk, 2 * head),
                "x",
                "yl",
            ).reshape(rows, 2 * head)
            return join(
                jnp.where(first, cots[:, :head], cots[:, head:]),
                jnp.where(first, cots[:, head:], cots[:, :head]),
            ), w_own, w_other
        return carry + (project(groups[n - 1], parts),)

    parts, (cot, _, _, *done) = gather_rounds(tokens, "x", "yl", token_work)
    half_tokens = join(*[x for x, _ in done])
    partial = join(*[y for _, y in done])

    kv_part = partial[:, 2 * head :]
    kv_sent = shift(lax.dynamic_slice_in_dim(kv_part, (1 - core) * half_rows, half_rows, 0), "pool", 1)
    kv_mine = lax.dynamic_slice_in_dim(kv_part, core * half_rows, half_rows, 0)
    kv = add(kv_mine, kv_sent)
    q_part = join(partial[:, :head], partial[:, head : 2 * head])
    q = add(q_part, shift(q_part, "pool", 1))

    def key_work(n, kvs, carry):
        if n == 0:
            return attention_stats(q, cot, kvs[(0, 0)], scale2, None)
        at = (slice(1, 4), slice(4, 7), slice(7, 8))[n - 1]
        return attention_stats(q, cot, join(*[kvs[k] for k in ORDER[at]]), scale2, carry)

    kvs, mine = gather_rounds(kv, "z", "yh", key_work)
    kv_all = join(*[kvs[k] for k in ORDER])
    other = shift(mine, "pool", 1)
    other_tokens = shift(half_tokens, "pool", 1)

    def key_grads(tiles, running):
        dkv, dq = attention_grads(q, cot, kv_all, tiles, mine, other, scale2, scaling, running)
        return {ORDER[t]: dkv[n * half_rows : (n + 1) * half_rows] for n, t in enumerate(tiles)}, dq

    pieces, dq_t = key_grads(range(5, 8), None)
    got_one = scatter_one(pieces, "z")
    more, dq_t = key_grads(range(2, 5), dq_t)
    pieces.update(more)
    got_one, dq_t = tie((got_one, dq_t))
    got_two = scatter_two(pieces, got_one, "z")
    more, dq_t = key_grads(range(0, 2), dq_t)
    pieces.update(more)
    got_two, dq_t = tie((got_two, dq_t))
    got_three = scatter_three(pieces, got_one, got_two, "z", "yh")
    dq_t = (dq_t * scaling).astype(BF16)
    dq_t = (widen(dq_t) + widen(shift(dq_t, "pool", 1))).reshape(2, rows // Q_TILE, head, Q_TILE)
    dq = dq_t.transpose(1, 3, 0, 2).reshape(rows, 2 * head).astype(BF16)

    def halves():
        near = lax.axis_index("yh") == core
        return jnp.where(near, other_tokens, half_tokens), jnp.where(near, half_tokens, other_tokens)

    far_tokens, near_tokens = halves()

    def term_of(x, grad):
        grad = jnp.where(owned, grad, jnp.zeros_like(grad))
        return lax.dot_general(x, grad, TN, preferred_element_type=F32).astype(BF16)

    far_q, near_q = term_of(far_tokens, dq), term_of(near_tokens, dq)
    got_three, dq, far_q, near_q = tie((got_three, dq, far_q, near_q))
    dkv = scatter_sum(pieces, got_three).astype(BF16)
    dkv_other = shift(dkv, "pool", 1)
    dkv_rows = join(jnp.where(first, dkv, dkv_other), jnp.where(first, dkv_other, dkv))
    grad_proj = jnp.concatenate([dq, dkv_rows], axis=1)
    zero = jnp.zeros_like(grad_proj)
    spread = jnp.concatenate(
        [jnp.where(owned, grad_proj, zero), jnp.where(owned, zero, grad_proj)], axis=1
    )
    w_both = jnp.concatenate([w_own, w_other], axis=1)

    def back_of(at):
        out = lax.dot_general(
            spread[at.start * chunk : at.stop * chunk], w_both, NT, preferred_element_type=F32
        ).astype(BF16)
        return {k: out[n * chunk : (n + 1) * chunk] for n, k in enumerate(ORDER[at])}

    def pieces_of(term_q, term_kv, twin):
        term = jnp.concatenate([term_q, term_kv], axis=1).reshape(4, half_width // 4, 4 * head)
        i = lax.axis_index("z")
        return {
            (d, twin): lax.dynamic_index_in_dim(term, (i + d) % 4, 0, keepdims=False) for d in range(4)
        }

    back = back_of(slice(5, 8))
    term = pieces_of(far_q, term_of(far_tokens, dkv_rows), 1)
    back_one = scatter_one(back, "x")
    term_one = scatter_one(term, "z")
    more_back = back_of(slice(0, 5))
    more_term = pieces_of(near_q, term_of(near_tokens, dkv_rows), 0)
    back_one, term_one, more_back, more_term = tie((back_one, term_one, more_back, more_term))
    back.update(more_back)
    term.update(more_term)
    back_two = scatter_two(back, back_one, "x")
    term_two = scatter_two(term, term_one, "z")
    back_two, term_two = tie((back_two, term_two))
    back_three = scatter_three(back, back_one, back_two, "x", "yl")
    term_three = scatter_three(term, term_one, term_two, "z", "yh")
    back_three, term_three = tie((back_three, term_three))
    grad_tokens = scatter_sum(back, back_three).astype(BF16)
    grad_weight = scatter_sum(term, term_three)
    return (grad_tokens, grad_weight[None])


def solution(mesh):
    fine = Mesh(mesh.devices.reshape(2, 2, 4, 4, 2), ("pool", "yh", "z", "x", "yl"))
    pb = ("yh", "z")
    ka = ("x", "yl")
    return jax.shard_map(
        shards,
        mesh=fine,
        in_specs=(P(pb + ka, "pool"), P(pb), P("pool", None, ka), P("pool", pb, ka)),
        out_specs=(P(pb + ka, "pool"), P("pool", pb, ka)),
        check_vma=False,
    )
```

```python
import math

import jax
import jax.numpy as jnp
from jax import lax
from jax.experimental import pallas as pl
from jax.experimental.pallas import tpu as pltpu
from jax.sharding import Mesh, PartitionSpec as P


F32 = jnp.float32
BF16 = jnp.bfloat16
NT = (((1,), (1,)), ((), ()))
TN = (((0,), (0,)), ((), ()))
NN = (((1,), (0,)), ((), ()))
KEY_TILE = 512
Q_TILE = 512
UNROLL = 4
ORDER = ((0, 0), (1, 0), (3, 0), (0, 1), (2, 0), (1, 1), (3, 1), (2, 1))
tie = lax.optimization_barrier


def shift(value, axis, step):
    count = lax.axis_size(axis)
    return lax.ppermute(value, axis, [(i, (i + step) % count) for i in range(count)])


def widen(value):
    return value.astype(F32)


def join(*values):
    return jnp.concatenate(values)


def add(x, y):
    return (widen(x) + widen(y)).astype(BF16)


def scatter_row(p, e, ring):
    return [shift(p[(d, e)], ring, step) for d, step in ((1, 1), (3, -1), (2, 2))]


def total(own, got):
    result = widen(own)
    for value in got:
        result = result + widen(value)
    return result


def stats_body(scale2, fresh, q_ref, o_ref, kv_ref, *refs):
    out_ref = refs[-1]

    @pl.when(pl.program_id(0) == 0)
    def _():
        if fresh:
            out_ref[:, 0:1, :] = jnp.full((out_ref.shape[0], 1, Q_TILE), -jnp.inf, F32)
            out_ref[:, 1:8, :] = jnp.zeros((out_ref.shape[0], 7, Q_TILE), F32)
        else:
            out_ref[...] = refs[0][...]

    keys = kv_ref[:, :128]
    values = kv_ref[:, 128:]

    def block(b, _):
        at = pl.ds(pl.multiple_of(b * Q_TILE, Q_TILE), Q_TILE)
        s = lax.dot_general(keys, q_ref[at, :], NT, preferred_element_type=F32)
        g = lax.dot_general(values, o_ref[at, :], NT, preferred_element_type=F32)
        old = out_ref[b, 0:1, :]
        new = jnp.maximum(old, jnp.max(s, axis=0, keepdims=True))
        fade = jnp.exp2((old - new) * scale2)
        e = jnp.exp2(s * scale2 - new * scale2)
        out_ref[b, 0:1, :] = new
        out_ref[b, 1:2, :] = fade * out_ref[b, 1:2, :] + jnp.sum(e, axis=0, keepdims=True)
        out_ref[b, 2:3, :] = fade * out_ref[b, 2:3, :] + jnp.sum(e * g, axis=0, keepdims=True)
        return _

    lax.fori_loop(0, out_ref.shape[0], block, 0, unroll=UNROLL)


def attention_stats(q, o, kv, scale2, running):
    count = kv.shape[0]
    blocks = q.shape[0] // Q_TILE
    shape = (blocks, 8, Q_TILE)
    whole = pl.BlockSpec(shape, lambda i: (0, 0, 0))
    fresh = running is None
    args = (q, o, kv) if fresh else (q, o, kv, running)
    return pl.pallas_call(
        lambda *refs: stats_body(scale2, fresh, *refs),
        grid=(count // KEY_TILE,),
        in_specs=[
            pl.BlockSpec(q.shape, lambda i: (0, 0)),
            pl.BlockSpec(o.shape, lambda i: (0, 0)),
            pl.BlockSpec((KEY_TILE, 256), lambda i: (i, 0)),
        ]
        + ([] if fresh else [whole]),
        out_specs=whole,
        out_shape=jax.ShapeDtypeStruct(shape, F32),
        name="attention_stats",
    )(*args)


def grads_body(scale2, scaling, fresh, q_ref, o_ref, kv_ref, mine_ref, other_ref, *refs):
    dkv_ref, dq_ref, row_ref, acc_ref = refs[-4:]

    @pl.when(pl.program_id(0) == 0)
    def _():
        for b in range(dq_ref.shape[0]):
            top_a = mine_ref[b, 0:1, :]
            top_b = other_ref[b, 0:1, :]
            top = jnp.maximum(top_a, top_b)
            fade_a = jnp.exp2((top_a - top) * scale2)
            fade_b = jnp.exp2((top_b - top) * scale2)
            total = mine_ref[b, 1:2, :] * fade_a + other_ref[b, 1:2, :] * fade_b
            mixed = mine_ref[b, 2:3, :] * fade_a + other_ref[b, 2:3, :] * fade_b
            row_ref[b, 0:1, :] = top * scale2 + jnp.log2(total)
            row_ref[b, 1:2, :] = mixed / total
        if fresh:
            dq_ref[...] = jnp.zeros_like(dq_ref)
        else:
            dq_ref[...] = refs[0][...]

    keys = kv_ref[:, :128]
    values = kv_ref[:, 128:]
    keys_t = keys.T
    acc_ref[...] = jnp.zeros_like(acc_ref)

    def block(b, _):
        at = pl.ds(pl.multiple_of(b * Q_TILE, Q_TILE), Q_TILE)
        q = q_ref[at, :]
        o = o_ref[at, :]
        s = lax.dot_general(keys, q, NT, preferred_element_type=F32)
        g = lax.dot_general(values, o, NT, preferred_element_type=F32)
        p = jnp.exp2(s * scale2 - row_ref[b, 0:1, :])
        ds = (p * (g - row_ref[b, 1:2, :])).astype(BF16)
        acc_ref[:, :128] += lax.dot_general(ds, q, NN, preferred_element_type=F32)
        acc_ref[:, 128:] += lax.dot_general(p.astype(BF16), o, NN, preferred_element_type=F32)
        dq_ref[b] += lax.dot_general(keys_t, ds, NN, preferred_element_type=F32)
        return _

    lax.fori_loop(0, dq_ref.shape[0], block, 0, unroll=UNROLL)
    dkv_ref[:, :128] = (acc_ref[:, :128] * scaling).astype(BF16)
    dkv_ref[:, 128:] = acc_ref[:, 128:].astype(BF16)


def attention_grads(q, o, kv, tiles, mine, other, scale2, scaling, running):
    start, count = tiles.start, len(tiles) * KEY_TILE
    blocks = q.shape[0] // Q_TILE
    shape = (blocks, 128, Q_TILE)
    fresh = running is None
    stats = pl.BlockSpec(mine.shape, lambda i: (0, 0, 0))
    whole = pl.BlockSpec(shape, lambda i: (0, 0, 0))
    args = (q, o, kv, mine, other) + (() if fresh else (running,))
    return pl.pallas_call(
        lambda *refs: grads_body(scale2, scaling, fresh, *refs),
        grid=(count // KEY_TILE,),
        in_specs=[
            pl.BlockSpec(q.shape, lambda i: (0, 0)),
            pl.BlockSpec(o.shape, lambda i: (0, 0)),
            pl.BlockSpec((KEY_TILE, 256), lambda i: (i + start, 0)),
            stats,
            stats,
        ]
        + ([] if fresh else [whole]),
        out_specs=[pl.BlockSpec((KEY_TILE, 256), lambda i: (i, 0)), whole],
        out_shape=[
            jax.ShapeDtypeStruct((count, 256), BF16),
            jax.ShapeDtypeStruct(shape, F32),
        ],
        scratch_shapes=[pltpu.VMEM((blocks, 8, Q_TILE), F32), pltpu.VMEM((KEY_TILE, 256), F32)],
        name="attention_grads",
    )(*args)


def rolled(value, ring, pair):
    i = lax.axis_index(ring)
    j = lax.axis_index(pair)
    value = lax.dynamic_slice_in_dim(jnp.concatenate([value, value]), i, 4, 0)
    value = lax.dynamic_slice_in_dim(jnp.concatenate([value, value], axis=1), j, 2, 1)
    return jnp.stack([value[k] for k in ORDER])


def shards(tokens, modality, proj_weight, out_grad):
    core = lax.axis_index("pool")
    first = core == 0
    head = out_grad.shape[2]
    scaling = 1.0 / math.sqrt(head)
    scale2 = scaling * math.log2(math.e)
    chunk, half_width = tokens.shape
    rows = 8 * chunk
    half_rows = rows // 2

    weight = proj_weight[0]
    w_own = lax.dynamic_slice_in_dim(weight, core * half_width, half_width, 0)
    w_other = shift(lax.dynamic_slice_in_dim(weight, (1 - core) * half_width, half_width, 0), "pool", 1)
    partner_grad = shift(out_grad[0], "pool", 1)

    owned = (rolled(modality.reshape(4, 2, chunk), "x", "yl").reshape(rows) == core)[:, None]

    def project(x, at):
        return jnp.where(
            owned[at : at + x.shape[0]],
            jnp.dot(x, w_own, preferred_element_type=F32),
            jnp.dot(x, w_other, preferred_element_type=F32),
        ).astype(BF16)

    h = chunk // 2
    t = chunk * 3 // 8
    own0, own1 = tokens[:h], tokens[h:]
    left0, right1, twin0 = shift(own0, "x", 1), shift(own1, "x", -1), shift(own0, "yl", 1)
    left1, right0, twin1 = shift(own1, "x", 1), shift(own0, "x", -1), shift(own1, "yl", 1)
    cots = rolled(
        jnp.concatenate([out_grad[0], partner_grad], axis=1).reshape(4, 2, chunk, 2 * head), "x", "yl"
    ).reshape(rows, 2 * head)
    cot = join(
        jnp.where(first, cots[:, :head], cots[:, head:]),
        jnp.where(first, cots[:, head:], cots[:, :head]),
    )
    left0, right1, cot = tie((left0, right1, cot))
    far0, far1 = shift(left0, "x", 1), shift(right1, "x", -1)
    left1, right0, twin0, twin1 = tie((left1, right0, twin0, twin1))
    twin_left1, twin_right0 = shift(left1, "yl", 1), shift(right0, "yl", 1)
    twin_left0, twin_right1 = shift(twin0, "x", 1), shift(twin1, "x", -1)
    x_near = join(own0, own1, right0, right1, left0, left1, twin0, twin1)
    near = project(x_near, 0)
    far0, far1, twin_left0, twin_left1, twin_right0, twin_right1, near = tie(
        (far0, far1, twin_left0, twin_left1, twin_right0, twin_right1, near)
    )
    last0, last2 = shift(twin_left0[:t], "x", 1), shift(twin_right1[h - t :], "x", -1)
    last1 = shift(join(far0[t:], far1[: h - t]), "yl", 1)
    x_far = join(
        far0, far1, twin_right0, twin_right1, twin_left0, twin_left1, last0, last1, last2
    )
    half_tokens = join(x_near, x_far)
    partial = join(near, project(x_far, half_rows))

    kv_part = partial[:, 2 * head :]
    kv_sent = shift(lax.dynamic_slice_in_dim(kv_part, (1 - core) * half_rows, half_rows, 0), "pool", 1)
    kv_mine = lax.dynamic_slice_in_dim(kv_part, core * half_rows, half_rows, 0)
    kv = add(kv_mine, kv_sent)
    q_part = join(partial[:, :head], partial[:, head : 2 * head])
    q = add(q_part, shift(q_part, "pool", 1))

    kv_twin = shift(kv, "yh", 1)
    kv_row = [shift(kv, "z", step) for step in (-1, 1, 2)]
    kv_twins = [shift(kv_twin, "z", step) for step in (-1, 1, 2)]
    kv_row = join(kv, *kv_row)
    mine = attention_stats(q, cot, kv_row, scale2, None)
    kv_twins = join(kv_twin, *kv_twins)
    mine = attention_stats(q, cot, kv_twins, scale2, mine)
    other = shift(mine, "pool", 1)
    other_tokens = shift(half_tokens, "pool", 1)

    pieces = {}
    dq_t = None

    def key_grads(e, tiles, running):
        dkv, dq = attention_grads(
            q, cot, kv_twins if e else kv_row, tiles, mine, other, scale2, scaling, running
        )
        for n, t in enumerate(tiles):
            pieces[((0, 1, 3, 2)[t], e)] = dkv[n * half_rows : (n + 1) * half_rows]
        return dq

    dq_t = key_grads(1, range(1, 4), None)
    got_twin = scatter_row(pieces, 1, "z")
    dq_t = key_grads(0, range(1, 4), dq_t)
    got_own = scatter_row(pieces, 0, "z")
    dq_t = key_grads(1, range(0, 1), dq_t)
    got_twin, dq_t = tie((got_twin, dq_t))
    crossed = shift(total(pieces[(0, 1)], got_twin).astype(BF16), "yh", 1)
    dq_t = key_grads(0, range(0, 1), dq_t)
    dq_t = (dq_t * scaling).astype(BF16)
    dq_t = (widen(dq_t) + widen(shift(dq_t, "pool", 1))).reshape(2, rows // Q_TILE, head, Q_TILE)
    dq = dq_t.transpose(1, 3, 0, 2).reshape(rows, 2 * head).astype(BF16)

    dkv = total(pieces[(0, 0)], got_own + [crossed]).astype(BF16)
    dkv_other = shift(dkv, "pool", 1)
    dkv_rows = join(jnp.where(first, dkv, dkv_other), jnp.where(first, dkv_other, dkv))
    grad_proj = jnp.concatenate([dq, dkv_rows], axis=1)
    zero = jnp.zeros_like(grad_proj)
    spread = jnp.concatenate(
        [jnp.where(owned, grad_proj, zero), jnp.where(owned, zero, grad_proj)], axis=1
    )
    w_both = jnp.concatenate([w_own, w_other], axis=1)

    def back_of(grads, at):
        out = lax.dot_general(
            grads[at.start * chunk : at.stop * chunk], w_both, NT, preferred_element_type=F32
        ).astype(BF16)
        return {k: out[n * chunk : (n + 1) * chunk] for n, k in enumerate(ORDER[at])}

    near_core = lax.axis_index("yh") == core

    def term_of(grads, twin):
        x = jnp.where(near_core == (twin == 0), half_tokens, other_tokens)
        term = lax.dot_general(x, grads[:, : 4 * head], TN, preferred_element_type=F32).astype(BF16)
        term = term.reshape(4, half_width // 4, 4 * head)
        i = lax.axis_index("z")
        return {
            (d, twin): lax.dynamic_index_in_dim(term, (i + d) % 4, 0, keepdims=False) for d in range(4)
        }

    back = back_of(spread, slice(5, 8))
    back_twin = scatter_row(back, 1, "x")
    term = term_of(spread, 1)
    term_twin = scatter_row(term, 1, "z")
    spread, term = tie((spread, term))
    back.update(back_of(spread, slice(0, 5)))
    back_own = scatter_row(back, 0, "x")
    spread, back = tie((spread, back))
    term.update(term_of(spread, 0))
    term_own = scatter_row(term, 0, "z")
    back_cross = shift(total(back[(0, 1)], back_twin).astype(BF16), "yl", 1)
    term_cross = shift(total(term[(0, 1)], term_twin).astype(BF16), "yh", 1)
    grad_tokens = total(back[(0, 0)], back_own + [back_cross]).astype(BF16)
    grad_weight = total(term[(0, 0)], term_own + [term_cross])
    return (grad_tokens, grad_weight[None])


def solution(mesh):
    fine = Mesh(mesh.devices.reshape(2, 2, 4, 4, 2), ("pool", "yh", "z", "x", "yl"))
    pb = ("yh", "z")
    ka = ("x", "yl")
    return jax.shard_map(
        shards,
        mesh=fine,
        in_specs=(P(pb + ka, "pool"), P(pb), P("pool", None, ka), P("pool", pb, ka)),
        out_specs=(P(pb + ka, "pool"), P("pool", pb, ka)),
        check_vma=False,
    )
```
